768 devices in a mesh: dp: 12 (over z_lo, x), seq: 32 (over y, z_hi), head: 2 (over core).
Axes of the slice: x: 4, y: 8, z: 12 (z_hi: 4, z_lo: 3; z = z_hi * 3 + z_lo), core: 2. Of those that a mesh axis runs over, the one named last changes fastest.
Arguments:
- q_img: bfloat16 [12, 5632, 1536], P('dp', 'seq', 'head'), may hold values from -51 to 51
- k_img: bfloat16 [12, 5632, 1536], P('dp', 'seq', 'head'), may hold values from -4 to 4
- v_img: bfloat16 [12, 5632, 1536], P('dp', 'seq', 'head'), may hold values from -6 to 6
- k_txt: bfloat16 [12, 512, 1536], P('dp', 'seq', 'head'), may hold values from -6 to 6
- v_txt: bfloat16 [12, 512, 1536], P('dp', 'seq', 'head'), may hold values from -6 to 6
- text_length: int32 [12, 2], P('dp'), may hold values from 1 to 256, as said below
- w_out: bfloat16 [1536, 3072], P('head'), may hold values from -4 to 4
- branch_gate: float32 [3072], P('dp'), may hold values from 0.5 to 2
Outputs:
- branch_out: bfloat16 [12, 5632, 3072], P('dp', 'seq', 'head')
The draws below stay inside these ranges and needn't reach their ends.
Inputs may be any that keep to these rules, and one draw needn't show every extreme that they name: `text_length`: some sample has all 256 text slots live.
All inputs are finite; a program needn't handle non-finite values.
Results may differ from the reference program's by a relative error of at most 0.014.
Values may be sent and summed in bfloat16 or wider, within the bound.
No kernel may reach another device: no remote copies, remote signals or barrier semaphores. Data moves between devices by JAX's collectives and lax.ppermute only.
A program may use at most 32 MiB of HBM per device.

```python
import math
import jax
import jax.numpy as jnp
from jax import lax

D = 3072
HEAD_DIM = 128
HEADS = 12
IMG_DEV = 176
TXT_DEV = 16
GROUPS = 12
IMG = 2816
TXT = 256
N_SEQ = 32


def shared_keys(key):
    shape = (GROUPS, 2 * IMG, HEADS * HEAD_DIM)
    return jax.random.truncated_normal(jax.random.fold_in(key, 102), -4.0, 4.0, shape, jnp.float32)


def draw_k_img(key, part):
    keys_drawn = shared_keys(key)
    return keys_drawn.astype(jnp.bfloat16)


def draw_q_img(key, part):
    shape = (GROUPS, 2 * IMG, HEADS * HEAD_DIM)
    base = jax.random.truncated_normal(jax.random.fold_in(key, 105), -4.0, 4.0, shape, jnp.float32)
    return base.astype(jnp.bfloat16)


def draw_text_length(key, part):
    lengths = jax.random.randint(jax.random.fold_in(key, 7), (GROUPS * 2,), 1, TXT + 1)
    fullest = jax.random.randint(jax.random.fold_in(key, 8), (), 0, GROUPS * 2)
    return lengths.at[fullest].set(TXT).astype(jnp.int32).reshape(GROUPS, 2)


def steps_of(key, shape, cuts, low, high):
    def one(dim, blocks):
        steps = jax.random.uniform(jax.random.fold_in(jax.random.fold_in(key, 6), dim), (blocks,), jnp.float32, low / len(cuts), high / len(cuts))
        return jnp.repeat(jnp.exp(steps), shape[dim] // blocks).reshape((-1,) + (1,) * (len(shape) - dim - 1))

    loudness = one(*cuts[0])
    for cut in cuts[1:]:
        loudness = loudness * one(*cut)
    return loudness


def gaussian(own_key, dims, spread, most, cuts=(), kind=jnp.bfloat16):
    gain = steps_of(own_key, dims, cuts, -0.22, 0.18) if cuts else 1.0
    entries = jax.random.normal(own_key, dims, jnp.float32) * spread * gain
    return jnp.minimum(jnp.maximum(entries, -most), most).astype(kind)


def setup_inputs(seed: int = 0) -> dict:
    key_of = jax.random.split(jax.random.key(seed), 9)
    q_img = draw_q_img(jax.random.fold_in(key_of[8], 71), 0)
    k_img = draw_k_img(jax.random.fold_in(key_of[8], 71), 0)
    v_img = gaussian(key_of[2], (GROUPS, 2 * IMG, HEADS * HEAD_DIM), 1.0, 6.0, ((0, 12), (1, 32), (2, 2)))
    k_txt = gaussian(key_of[3], (GROUPS, 2 * TXT, HEADS * HEAD_DIM), 1.0, 6.0, ((0, 12), (1, 32), (2, 2)))
    v_txt = gaussian(key_of[4], (GROUPS, 2 * TXT, HEADS * HEAD_DIM), 1.0, 6.0, ((0, 12), (1, 32), (2, 2)))
    text_length = draw_text_length(jax.random.fold_in(key_of[8], 71), 0)
    w_out = gaussian(key_of[6], (HEADS * HEAD_DIM, D), (max(1, HEADS * HEAD_DIM * 4 // (IMG + TXT))) ** -0.5, 4.0, ((0, 2),))
    branch_gate = jnp.clip(jnp.exp(math.log(2.0) - 1.3862944 * jax.random.uniform(key_of[7], (D,), jnp.float32) ** steps_of(key_of[7], (D,), ((0, 12),), -0.2, 0.2)), 0.5, 2.0)
    return {"q_img": q_img, "k_img": k_img, "v_img": v_img, "k_txt": k_txt, "v_txt": v_txt, "text_length": text_length, "w_out": w_out, "branch_gate": branch_gate}


def to_samples(whole, per):
    groups = whole.shape[0]
    width = whole.shape[2]
    return whole.reshape(groups, N_SEQ // 2, 2, per, width).transpose(0, 2, 1, 3, 4).reshape(groups * 2, N_SEQ // 2 * per, width)

def text_samples(whole):
    groups = whole.shape[0]
    width = whole.shape[2]
    half_rows = TXT_DEV // 2
    return whole.reshape(groups, N_SEQ, 2, half_rows, width).transpose(0, 2, 1, 3, 4).reshape(groups * 2, N_SEQ * half_rows, width)

def reference(q_img, k_img, v_img, k_txt, v_txt, text_length, w_out, branch_gate):
    scaling = 1.0 / math.sqrt(HEAD_DIM)
    usable_image = jnp.ones((IMG,), dtype=bool)
    groups = q_img.shape[0]

    def one_sample(packed):
        queries, img_keys, img_values, txt_keys, txt_values, live_text = packed
        all_keys = jnp.concatenate([img_keys, txt_keys], axis=0)
        all_values = jnp.concatenate([img_values, txt_values], axis=0)
        usable = jnp.concatenate([usable_image, jnp.arange(TXT, dtype=jnp.int32) < live_text])

        def one_head(head):
            offset = (head * HEAD_DIM).astype(jnp.int32)
            head_queries = lax.dynamic_slice_in_dim(queries, offset, HEAD_DIM, 1)
            head_keys = lax.dynamic_slice_in_dim(all_keys, offset, HEAD_DIM, 1)
            head_values = lax.dynamic_slice_in_dim(all_values, offset, HEAD_DIM, 1)
            scores = jnp.dot(head_queries, head_keys.T, preferred_element_type=jnp.float32) * scaling
            scores = jnp.where(usable[None, :], scores, -jnp.inf)
            largest = lax.optimization_barrier(jnp.max(scores, axis=1, keepdims=True))
            weights = jnp.exp(scores - largest)
            totals = lax.optimization_barrier(jnp.sum(weights, axis=1, keepdims=True))
            return jnp.dot(weights.astype(jnp.bfloat16), head_values, preferred_element_type=jnp.float32) / totals
        per_head = lax.map(one_head, jnp.arange(HEADS, dtype=jnp.int32))
        attended = jnp.transpose(per_head, (1, 0, 2)).reshape(IMG, HEADS * HEAD_DIM).astype(jnp.bfloat16)
        projected = jnp.dot(attended, w_out, preferred_element_type=jnp.float32)
        return (projected * branch_gate).astype(jnp.bfloat16)
    packed = (to_samples(q_img, IMG_DEV), to_samples(k_img, IMG_DEV), to_samples(v_img, IMG_DEV), text_samples(k_txt), text_samples(v_txt), text_length.reshape(groups * 2))
    results = lax.map(one_sample, packed)
    return results.reshape(groups, 2, N_SEQ // 2, IMG_DEV, D).transpose(0, 2, 1, 3, 4).reshape(groups, 2 * IMG, D)
```

```python
import functools
import math

import jax
import jax.numpy as jnp
from jax import lax
from jax.experimental import pallas as pl
from jax.experimental.pallas import tpu as pltpu
from jax.sharding import PartitionSpec as P


HEAD_DIM = 128
PLANES = 4
BF16 = jnp.bfloat16
F32 = jnp.float32
VMEM = pl.BlockSpec(memory_space=pltpu.VMEM)
SMEM = pl.BlockSpec(memory_space=pltpu.SMEM)


def place():
    position = lax.axis_index("seq")
    y = lax.div(position, PLANES)
    plane = lax.rem(position, PLANES)
    return y, plane, lax.rem(plane, 2), lax.div(plane, 2)


def move(array, rows, by_y, by_plane):
    pairs = [
        (y * PLANES + z, (y + by_y) % rows * PLANES + (z + by_plane) % PLANES)
        for y in range(rows)
        for z in range(PLANES)
    ]
    return lax.ppermute(array, "seq", pairs)


def swap_cores(array):
    return lax.ppermute(array, "head", [(0, 1), (1, 0)])


def call(body, out_shape, in_specs, cost, limit=24 << 20):
    flops, moved, exps = cost
    return pl.pallas_call(
        body,
        out_shape=out_shape,
        in_specs=in_specs,
        out_specs=jax.tree.map(lambda _: VMEM, out_shape),
        compiler_params=pltpu.CompilerParams(vmem_limit_bytes=limit),
        cost_estimate=pl.CostEstimate(
            flops=flops, bytes_accessed=moved, transcendentals=exps
        ),
    )


def text_body(kt, vt, out):
    text = out.shape[0]
    width = kt.shape[2]
    _, _, sample, _ = place()
    rows = pl.ds(pl.multiple_of((1 - sample) * text, text), text)
    out[:, :width] = kt[0, rows, :]
    out[:, width:] = vt[0, rows, :]


def pack_body(k, v, kt, vt, got, out):
    rows, width = k.shape[1:]
    text = got.shape[0]
    _, _, sample, _ = place()
    mine = pl.ds(pl.multiple_of(sample * text, text), text)
    out[:rows, :width] = k[0]
    out[:rows, width:] = v[0]
    out[rows : rows + text, :width] = kt[0, mine, :]
    out[rows : rows + text, width:] = vt[0, mine, :]
    out[rows + text :, :] = got[...]


def attend_body(kinds, first, last, row_count, *refs):
    live_ref, q_near, q_far = refs[:3]
    refs = refs[3:]
    blocks, refs = refs[: len(kinds)], refs[len(kinds) :]
    if not first:
        acc_in, stat_in = refs[:2]
        refs = refs[2:]
    y, plane, sample, _ = place()
    live = live_ref[0, sample]
    rows, half = q_near.shape[1:]
    heads = half // HEAD_DIM
    width = pl.cdiv(2 * rows, 128) * 128
    factor = math.log2(math.e) / math.sqrt(HEAD_DIM)
    pad = jnp.zeros((width - 2 * rows, HEAD_DIM), BF16)
    logs = []
    for h in range(heads):
        cols = slice(h * HEAD_DIM, (h + 1) * HEAD_DIM)
        vals = slice(half + h * HEAD_DIM, half + (h + 1) * HEAD_DIM)
        queries = jnp.concatenate([q_far[0, :, cols], q_near[0, :, cols], pad], axis=0)
        scores = []
        for (by_y, at), block in zip(kinds, blocks, strict=True):
            s = lax.dot_general(
                block[:, cols], queries, (((1,), (1,)), ((), ())), preferred_element_type=F32
            )
            count = block.shape[0]
            text = at + count - rows
            if text > 0:
                eighth = text // 2
                index = lax.broadcasted_iota(jnp.int32, (text, width), 0)
                origin = lax.rem(plane + lax.div(index, eighth), PLANES)
                slot = (
                    lax.rem(y + by_y, row_count) * (PLANES * eighth)
                    + origin * eighth
                    + lax.rem(index, eighth)
                )
                tail = jnp.where(slot < live, s[count - text :], -1e30)
                s = jnp.concatenate([s[: count - text], tail], axis=0)
            scores.append(s)
        top = functools.reduce(
            jnp.maximum, [jnp.max(s, axis=0, keepdims=True) for s in scores]
        )
        if not first:
            old = stat_in[h : h + 1, :]
            top = jnp.maximum(top, old)
            fade = jnp.exp2((old - top) * factor)
        shift = top * factor
        total = None
        acc = None
        for s, block in zip(scores, blocks, strict=True):
            w = jnp.exp2(s * factor - shift)
            part = jnp.sum(w, axis=0, keepdims=True)
            total = part if total is None else total + part
            out = lax.dot_general(
                block[:, vals],
                w.astype(BF16),
                (((0,), (0,)), ((), ())),
                preferred_element_type=F32,
            )
            acc = out if acc is None else acc + out
        span = slice(h * HEAD_DIM, (h + 1) * HEAD_DIM)
        if not first:
            total = total + fade * stat_in[heads + h : heads + h + 1, :]
            acc = acc + fade * acc_in[span, :]
        if last:
            far_out, near_out, log_out = refs
            result = jnp.transpose(acc / total)
            far_out[:rows, cols] = result[:rows].astype(BF16)
            near_out[:, cols] = result[rows : 2 * rows]
            logs.append(shift + jnp.log2(total))
        else:
            acc_out, stat_out = refs
            acc_out[span, :] = acc
            stat_out[h : h + 1, :] = top
            stat_out[heads + h : heads + h + 1, :] = total
    if last:
        log = jnp.concatenate(logs + [jnp.zeros((8 - heads, width), F32)], axis=0)
        log_out[...] = log
        rest = log
        for n in range(3):
            term = rest.astype(BF16)
            rest = rest - term.astype(F32)
            far_out[rows:, n * 256 : (n + 1) * 256] = term[:, :256]


def attend(row_count, live, q_near, q_far, blocks, state, last):
    rows, half = q_near.shape[1:]
    heads = half // HEAD_DIM
    width = pl.cdiv(2 * rows, 128) * 128
    kinds = tuple((by_y, at) for _, by_y, at in blocks)
    if last:
        out_shape = (
            jax.ShapeDtypeStruct((rows + 8, half), BF16),
            jax.ShapeDtypeStruct((rows, half), F32),
            jax.ShapeDtypeStruct((8, width), F32),
        )
    else:
        out_shape = (
            jax.ShapeDtypeStruct((half, width), F32),
            jax.ShapeDtypeStruct((16, width), F32),
        )
    keys = sum(b.shape[0] for b, _, _ in blocks)
    args = [live, q_near, q_far] + [b for b, _, _ in blocks] + list(state or ())
    return call(
        functools.partial(attend_body, kinds, state is None, last, row_count),
        out_shape,
        [SMEM] + [VMEM] * (len(args) - 1),
        (4 * keys * width * half, sum(a.size * 2 for a in args), keys * width * heads),
    )(*args)


def merge_body(got, near, log, out):
    rows, half = near.shape
    terms = [got[rows:, n * 256 : (n + 1) * 256].astype(F32) for n in range(3)]
    theirs = jnp.transpose(terms[0] + terms[1] + terms[2])
    mine = jnp.transpose(log[...])
    for h in range(half // HEAD_DIM):
        cols = slice(h * HEAD_DIM, (h + 1) * HEAD_DIM)
        a = mine[rows : 2 * rows, h : h + 1]
        b = theirs[:rows, h : h + 1]
        share = 1.0 / (1.0 + jnp.exp2(jnp.minimum(b - a, 126.0)))
        out[:, cols] = (
            near[:, cols] * share + got[:rows, cols].astype(F32) * (1.0 - share)
        ).astype(BF16)


def project_first_body(mine, w_own, out):
    out[...] = jnp.dot(mine[...], w_own[...], preferred_element_type=F32)


def project_last_body(x_size, partial, theirs, w_got, gates, out):
    total = partial[...] + jnp.dot(theirs[...], w_got[...], preferred_element_type=F32)
    blocks, _, gate_width = gates.shape
    z_size = blocks // x_size
    me = lax.axis_index("dp")
    first = lax.axis_index("head") * (blocks // 2)
    for j in range(blocks // 2):
        by_x = lax.rem(lax.rem(me, x_size) - lax.rem(first + j, x_size) + x_size, x_size)
        by_z = lax.rem(lax.div(me, x_size) - lax.div(first + j, x_size) + z_size, z_size)
        cols = slice(j * gate_width, (j + 1) * gate_width)
        out[0, :, cols] = (total[:, cols] * gates[by_z * x_size + by_x]).astype(BF16)


def gather_gates(gate, x_size, z_size):
    def along(array, by_z, by_x):
        pairs = [
            (z * x_size + x, (z + by_z) % z_size * x_size + (x + by_x) % x_size)
            for z in range(z_size)
            for x in range(x_size)
        ]
        return lax.ppermute(array, "dp", pairs)

    held = gate.reshape(1, 1, gate.shape[0])
    step = 1
    while step < x_size:
        held = jnp.concatenate([held, along(held, 0, step)], axis=0)
        step *= 2
    return jnp.concatenate([held] + [along(held, i, 0) for i in range(1, z_size)], axis=0)


def per_device(q_img, k_img, v_img, k_txt, v_txt, text_length, w_out, branch_gate):
    row_count = lax.axis_size("seq") // PLANES
    rows, width = q_img.shape[1:]
    text = k_txt.shape[1] // 2

    def shape(*dims):
        return jax.ShapeDtypeStruct(dims, BF16)

    t_send = call(
        text_body, shape(text, 2 * width), [VMEM] * 2, (0, 8 * text * width, 0)
    )(k_txt, v_txt)
    t_got = move(t_send, row_count, 0, -1)
    block = call(
        pack_body, shape(rows + 2 * text, 2 * width), [VMEM] * 5, (0, 8 * rows * width, 0)
    )(k_img, v_img, k_txt, v_txt, t_got)
    q_got = move(q_img, row_count, 0, 2)

    up, down = [block], [block]
    for _ in range(1, 4):
        up.append(move(up[-1], row_count, 1, 0))
        down.append(move(down[-1], row_count, -1, 0))
    cut = (rows + 2 * text) // 2
    up.append(move(up[3][:cut], row_count, 1, 0))
    down.append(move(down[3][cut:], row_count, -1, 0))

    groups = [
        [(block, 0, 0), (up[1], -1, 0), (down[1], 1, 0)],
        [(up[2], -2, 0), (down[2], 2, 0)],
        [(up[3], -3, 0), (down[3], 3, 0)],
        [(up[4], -4, 0), (down[4], 4, cut)],
    ]
    state = None
    for n, group in enumerate(groups):
        blocks = [(b, by % row_count, at) for b, by, at in group]
        state = attend(row_count, text_length, q_img, q_got, blocks, state, n == len(groups) - 1)
    o_far, o_near, o_log = state

    core = lax.axis_index("head")
    out_width = w_out.shape[1] // 2
    w_send = lax.dynamic_slice_in_dim(w_out, (1 - core) * out_width, out_width, 1)
    w_own = lax.dynamic_slice_in_dim(w_out, core * out_width, out_width, 1)
    w_got = swap_cores(w_send)
    gates = gather_gates(branch_gate, 4, lax.axis_size("dp") // 4)

    o_got = move(o_far, row_count, 0, 2)
    mine = call(
        merge_body, shape(rows, width), [VMEM] * 3, (0, 8 * rows * width, 0)
    )(o_got, o_near, o_log)
    theirs = swap_cores(mine)
    partial = call(
        project_first_body,
        jax.ShapeDtypeStruct((rows, out_width), F32),
        [VMEM] * 2,
        (2 * rows * width * out_width, 2 * width * out_width, 0),
    )(mine, w_own)
    return call(
        functools.partial(project_last_body, 4),
        shape(1, rows, out_width),
        [VMEM] * 4,
        (2 * rows * width * out_width, 2 * width * out_width, 0),
    )(partial, theirs, w_got, gates)


def solution(mesh):
    in_specs = (
        P("dp", "seq", "head"),
        P("dp", "seq", "head"),
        P("dp", "seq", "head"),
        P("dp", "seq", "head"),
        P("dp", "seq", "head"),
        P("dp", None),
        P("head", None),
        P("dp"),
    )
    out_specs = P("dp", "seq", "head")
    return jax.shard_map(
        per_device, mesh=mesh, in_specs=in_specs, out_specs=out_specs, check_vma=False
    )
```

```python
import functools
import math

import jax
import jax.numpy as jnp
from jax import lax
from jax.experimental import pallas as pl
from jax.experimental.pallas import tpu as pltpu
from jax.sharding import PartitionSpec as P


HEAD_DIM = 128
PLANES = 4
BF16 = jnp.bfloat16
F32 = jnp.float32
VMEM = pl.BlockSpec(memory_space=pltpu.VMEM)
SMEM = pl.BlockSpec(memory_space=pltpu.SMEM)
ANY = pl.BlockSpec(memory_space=pl.ANY)


def place():
    position = lax.axis_index("seq")
    y = lax.div(position, PLANES)
    plane = lax.rem(position, PLANES)
    return y, plane, lax.rem(plane, 2), lax.div(plane, 2)


def move(array, rows, by_y, by_plane):
    pairs = [
        (y * PLANES + z, (y + by_y) % rows * PLANES + (z + by_plane) % PLANES)
        for y in range(rows)
        for z in range(PLANES)
    ]
    return lax.ppermute(array, "seq", pairs)


def swap_cores(array):
    return lax.ppermute(array, "head", [(0, 1), (1, 0)])


def call(body, out_shape, in_specs, cost, limit=24 << 20, copies=0):
    flops, moved, exps = cost
    return pl.pallas_call(
        body,
        out_shape=out_shape,
        in_specs=in_specs,
        out_specs=jax.tree.map(lambda _: VMEM, out_shape),
        scratch_shapes=[pltpu.SemaphoreType.DMA((copies,))] if copies else [],
        compiler_params=pltpu.CompilerParams(vmem_limit_bytes=limit),
        cost_estimate=pl.CostEstimate(
            flops=flops, bytes_accessed=moved, transcendentals=exps
        ),
    )


def text_body(kt, vt, out, sems):
    text = out.shape[0]
    width = kt.shape[2]
    _, _, sample, _ = place()
    rows = pl.ds(pl.multiple_of((1 - sample) * text, text), text)
    copies = [
        pltpu.make_async_copy(kt.at[0, rows, :], out.at[:, :width], sems.at[0]),
        pltpu.make_async_copy(vt.at[0, rows, :], out.at[:, width:], sems.at[1]),
    ]
    for copy in copies:
        copy.start()
    for copy in copies:
        copy.wait()


def pack_body(k, v, kt, vt, got, out, sems):
    rows, width = k.shape[1:]
    text = got.shape[0]
    _, _, sample, _ = place()
    mine = pl.ds(pl.multiple_of(sample * text, text), text)
    own = pl.ds(rows, text)
    copies = [
        pltpu.make_async_copy(k.at[0], out.at[:rows, :width], sems.at[0]),
        pltpu.make_async_copy(v.at[0], out.at[:rows, width:], sems.at[1]),
        pltpu.make_async_copy(kt.at[0, mine, :], out.at[own, :width], sems.at[2]),
        pltpu.make_async_copy(vt.at[0, mine, :], out.at[own, width:], sems.at[3]),
    ]
    for copy in copies:
        copy.start()
    out[rows + text :, :] = got[...]
    for copy in copies:
        copy.wait()


def attend_body(kinds, first, last, row_count, *refs):
    live_ref, q_near, q_far = refs[:3]
    refs = refs[3:]
    blocks, refs = refs[: len(kinds)], refs[len(kinds) :]
    if not first:
        acc_in, stat_in = refs[:2]
        refs = refs[2:]
    y, plane, sample, _ = place()
    live = live_ref[0, sample]
    rows, half = q_near.shape[1:]
    heads = half // HEAD_DIM
    width = pl.cdiv(2 * rows, 128) * 128
    factor = math.log2(math.e) / math.sqrt(HEAD_DIM)
    pad = jnp.zeros((width - 2 * rows, HEAD_DIM), BF16)
    logs = []
    for h in range(heads):
        cols = slice(h * HEAD_DIM, (h + 1) * HEAD_DIM)
        vals = slice(half + h * HEAD_DIM, half + (h + 1) * HEAD_DIM)
        queries = jnp.concatenate([q_far[0, :, cols], q_near[0, :, cols], pad], axis=0)
        scores = []
        for (by_y, at), block in zip(kinds, blocks, strict=True):
            s = lax.dot_general(
                block[:, cols], queries, (((1,), (1,)), ((), ())), preferred_element_type=F32
            )
            count = block.shape[0]
            text = at + count - rows
            if text > 0:
                eighth = text // 2
                index = lax.broadcasted_iota(jnp.int32, (text, width), 0)
                origin = lax.rem(plane + lax.div(index, eighth), PLANES)
                slot = (
                    lax.rem(y + by_y, row_count) * (PLANES * eighth)
                    + origin * eighth
                    + lax.rem(index, eighth)
                )
                tail = jnp.where(slot < live, s[count - text :], -1e30)
                s = jnp.concatenate([s[: count - text], tail], axis=0)
            scores.append(s)
        top = functools.reduce(
            jnp.maximum, [jnp.max(s, axis=0, keepdims=True) for s in scores]
        )
        if not first:
            old = stat_in[h : h + 1, :]
            top = jnp.maximum(top, old)
            fade = jnp.exp2((old - top) * factor)
        shift = top * factor
        total = None
        acc = None
        for s, block in zip(scores, blocks, strict=True):
            w = jnp.exp2(s * factor - shift)
            part = jnp.sum(w, axis=0, keepdims=True)
            total = part if total is None else total + part
            out = lax.dot_general(
                block[:, vals],
                w.astype(BF16),
                (((0,), (0,)), ((), ())),
                preferred_element_type=F32,
            )
            acc = out if acc is None else acc + out
        span = slice(h * HEAD_DIM, (h + 1) * HEAD_DIM)
        if not first:
            total = total + fade * stat_in[heads + h : heads + h + 1, :]
            acc = acc + fade * acc_in[span, :]
        if last:
            far_out, near_out, log_out = refs
            result = jnp.transpose(acc / total)
            far_out[:rows, cols] = result[:rows].astype(BF16)
            near_out[:, cols] = result[rows : 2 * rows]
            logs.append(shift + jnp.log2(total))
        else:
            acc_out, stat_out = refs
            acc_out[span, :] = acc
            stat_out[h : h + 1, :] = top
            stat_out[heads + h : heads + h + 1, :] = total
    if last:
        log = jnp.concatenate(logs + [jnp.zeros((8 - heads, width), F32)], axis=0)
        log_out[...] = log
        rest = log
        for n in range(3):
            term = rest.astype(BF16)
            rest = rest - term.astype(F32)
            far_out[rows:, n * 256 : (n + 1) * 256] = term[:, :256]


def attend(row_count, live, q_near, q_far, blocks, state, last):
    rows, half = q_near.shape[1:]
    heads = half // HEAD_DIM
    width = pl.cdiv(2 * rows, 128) * 128
    kinds = tuple((by_y, at) for _, by_y, at in blocks)
    if last:
        out_shape = (
            jax.ShapeDtypeStruct((rows + 8, half), BF16),
            jax.ShapeDtypeStruct((rows, half), F32),
            jax.ShapeDtypeStruct((8, width), F32),
        )
    else:
        out_shape = (
            jax.ShapeDtypeStruct((half, width), F32),
            jax.ShapeDtypeStruct((16, width), F32),
        )
    keys = sum(b.shape[0] for b, _, _ in blocks)
    args = [live, q_near, q_far] + [b for b, _, _ in blocks] + list(state or ())
    return call(
        functools.partial(attend_body, kinds, state is None, last, row_count),
        out_shape,
        [SMEM] + [VMEM] * (len(args) - 1),
        (4 * keys * width * half, sum(a.size * 2 for a in args), keys * width * heads),
    )(*args)


def merge_body(x_size, got, near, log, gates, out, gate_out):
    blocks, _, gate_width = gates.shape
    z_size = blocks // x_size
    me = lax.axis_index("dp")
    first = lax.axis_index("head") * (blocks // 2)
    for j in range(blocks // 2):
        by_x = lax.rem(lax.rem(me, x_size) - lax.rem(first + j, x_size) + x_size, x_size)
        by_z = lax.rem(lax.div(me, x_size) - lax.div(first + j, x_size) + z_size, z_size)
        gate_out[:, j * gate_width : (j + 1) * gate_width] = gates[by_z * x_size + by_x]
    rows, half = near.shape
    terms = [got[rows:, n * 256 : (n + 1) * 256].astype(F32) for n in range(3)]
    theirs = jnp.transpose(terms[0] + terms[1] + terms[2])
    mine = jnp.transpose(log[...])
    for h in range(half // HEAD_DIM):
        cols = slice(h * HEAD_DIM, (h + 1) * HEAD_DIM)
        a = mine[rows : 2 * rows, h : h + 1]
        b = theirs[:rows, h : h + 1]
        share = 1.0 / (1.0 + jnp.exp2(jnp.minimum(b - a, 126.0)))
        out[:, cols] = (
            near[:, cols] * share + got[:rows, cols].astype(F32) * (1.0 - share)
        ).astype(BF16)


def project_first_body(mine, w_own, out):
    out[...] = jnp.dot(mine[...], w_own[...], preferred_element_type=F32)


def project_last_body(partial, theirs, w_got, gate, out):
    total = partial[...] + jnp.dot(theirs[...], w_got[...], preferred_element_type=F32)
    out[0] = (total * gate[...]).astype(BF16)


def gather_gates(gate, x_size, z_size):
    def along(array, by_z, by_x):
        pairs = [
            (z * x_size + x, (z + by_z) % z_size * x_size + (x + by_x) % x_size)
            for z in range(z_size)
            for x in range(x_size)
        ]
        return lax.ppermute(array, "dp", pairs)

    held = gate.reshape(1, 1, gate.shape[0])
    step = 1
    while step < x_size:
        held = jnp.concatenate([held, along(held, 0, step)], axis=0)
        step *= 2
    return jnp.concatenate([held] + [along(held, i, 0) for i in range(1, z_size)], axis=0)


def per_device(q_img, k_img, v_img, k_txt, v_txt, text_length, w_out, branch_gate):
    row_count = lax.axis_size("seq") // PLANES
    rows, width = q_img.shape[1:]
    text = k_txt.shape[1] // 2

    def shape(*dims):
        return jax.ShapeDtypeStruct(dims, BF16)

    t_send = call(
        text_body, shape(text, 2 * width), [ANY] * 2, (0, 8 * text * width, 0), copies=2
    )(k_txt, v_txt)
    t_got = move(t_send, row_count, 0, -1)
    block = call(
        pack_body,
        shape(rows + 2 * text, 2 * width),
        [ANY] * 4 + [VMEM],
        (0, 8 * rows * width, 0),
        copies=4,
    )(k_img, v_img, k_txt, v_txt, t_got)
    q_got = move(q_img, row_count, 0, 2)

    up, down = [block], [block]
    for _ in range(1, 4):
        up.append(move(up[-1], row_count, 1, 0))
        down.append(move(down[-1], row_count, -1, 0))
    cut = (rows + 2 * text) // 2
    up.append(move(up[3][:cut], row_count, 1, 0))
    down.append(move(down[3][cut:], row_count, -1, 0))

    groups = [
        [(block, 0, 0), (up[1], -1, 0), (down[1], 1, 0)],
        [(up[2], -2, 0), (down[2], 2, 0)],
        [(up[3], -3, 0), (down[3], 3, 0)],
        [(up[4], -4, 0), (down[4], 4, cut)],
    ]
    state = None
    for n, group in enumerate(groups):
        blocks = [(b, by % row_count, at) for b, by, at in group]
        state = attend(row_count, text_length, q_img, q_got, blocks, state, n == len(groups) - 1)
    o_far, o_near, o_log = state

    core = lax.axis_index("head")
    out_width = w_out.shape[1] // 2
    w_send = lax.dynamic_slice_in_dim(w_out, (1 - core) * out_width, out_width, 1)
    w_own = lax.dynamic_slice_in_dim(w_out, core * out_width, out_width, 1)
    w_got = swap_cores(w_send)
    gates = gather_gates(branch_gate, 4, lax.axis_size("dp") // 4)

    o_got = move(o_far, row_count, 0, 2)
    mine, gate = call(
        functools.partial(merge_body, 4),
        (shape(rows, width), jax.ShapeDtypeStruct((1, out_width), F32)),
        [VMEM] * 4,
        (0, 8 * rows * width, 0),
    )(o_got, o_near, o_log, gates)
    theirs = swap_cores(mine)
    partial = call(
        project_first_body,
        jax.ShapeDtypeStruct((rows, out_width), F32),
        [VMEM] * 2,
        (2 * rows * width * out_width, 2 * width * out_width, 0),
    )(mine, w_own)
    return call(
        project_last_body,
        shape(1, rows, out_width),
        [VMEM] * 4,
        (2 * rows * width * out_width, 2 * width * out_width, 0),
    )(partial, theirs, w_got, gate)


def solution(mesh):
    in_specs = (
        P("dp", "seq", "head"),
        P("dp", "seq", "head"),
        P("dp", "seq", "head"),
        P("dp", "seq", "head"),
        P("dp", "seq", "head"),
        P("dp", None),
        P("head", None),
        P("dp"),
    )
    out_specs = P("dp", "seq", "head")
    return jax.shard_map(
        per_device, mesh=mesh, in_specs=in_specs, out_specs=out_specs, check_vma=False
    )
```

```python
import functools
import math

import jax
import jax.numpy as jnp
from jax import lax
from jax.experimental import pallas as pl
from jax.experimental.pallas import tpu as pltpu
from jax.sharding import PartitionSpec as P


HEAD_DIM = 128
PLANES = 4
BF16 = jnp.bfloat16
F32 = jnp.float32
VMEM = pl.BlockSpec(memory_space=pltpu.VMEM)
SMEM = pl.BlockSpec(memory_space=pltpu.SMEM)
HBM = pl.BlockSpec(memory_space=pltpu.HBM)


def place():
    position = lax.axis_index("seq")
    y = lax.div(position, PLANES)
    plane = lax.rem(position, PLANES)
    return y, plane, lax.rem(plane, 2), lax.div(plane, 2)


def move(array, rows, by_y, by_plane):
    pairs = [
        (y * PLANES + z, (y + by_y) % rows * PLANES + (z + by_plane) % PLANES)
        for y in range(rows)
        for z in range(PLANES)
    ]
    return lax.ppermute(array, "seq", pairs)


def swap_cores(array):
    return lax.ppermute(array, "head", [(0, 1), (1, 0)])


def call(body, out_shape, in_specs, cost, limit=12 << 20, copies=0):
    flops, moved, exps = cost
    return pl.pallas_call(
        body,
        out_shape=out_shape,
        in_specs=in_specs,
        out_specs=jax.tree.map(lambda _: VMEM, out_shape),
        scratch_shapes=[pltpu.SemaphoreType.DMA((copies,))] if copies else [],
        compiler_params=pltpu.CompilerParams(vmem_limit_bytes=limit),
        cost_estimate=pl.CostEstimate(
            flops=flops, bytes_accessed=moved, transcendentals=exps
        ),
    )


def text_body(kt, vt, out, sems):
    text = out.shape[0]
    width = kt.shape[2]
    _, _, sample, _ = place()
    rows = pl.ds(pl.multiple_of((1 - sample) * text, text), text)
    copies = [
        pltpu.make_async_copy(kt.at[0, rows, :], out.at[:, :width], sems.at[0]),
        pltpu.make_async_copy(vt.at[0, rows, :], out.at[:, width:], sems.at[1]),
    ]
    for copy in copies:
        copy.start()
    for copy in copies:
        copy.wait()


def pack_body(k, v, kt, vt, got, out, sems):
    rows, width = k.shape[1:]
    text = got.shape[0]
    _, _, sample, _ = place()
    mine = pl.ds(pl.multiple_of(sample * text, text), text)
    own = pl.ds(rows, text)
    copies = [
        pltpu.make_async_copy(k.at[0], out.at[:rows, :width], sems.at[0]),
        pltpu.make_async_copy(v.at[0], out.at[:rows, width:], sems.at[1]),
        pltpu.make_async_copy(kt.at[0, mine, :], out.at[own, :width], sems.at[2]),
        pltpu.make_async_copy(vt.at[0, mine, :], out.at[own, width:], sems.at[3]),
    ]
    for copy in copies:
        copy.start()
    out[rows + text :, :] = got[...]
    for copy in copies:
        copy.wait()


def attend_body(kinds, first, last, row_count, *refs):
    live_ref, q_near, q_far = refs[:3]
    refs = refs[3:]
    blocks, refs = refs[: len(kinds)], refs[len(kinds) :]
    if not first:
        acc_in, stat_in = refs[:2]
        refs = refs[2:]
    y, plane, sample, _ = place()
    live = live_ref[0, sample]
    rows, half = q_near.shape[1:]
    heads = half // HEAD_DIM
    width = pl.cdiv(2 * rows, 128) * 128
    factor = math.log2(math.e) / math.sqrt(HEAD_DIM)
    pad = jnp.zeros((width - 2 * rows, HEAD_DIM), BF16)
    logs = []
    for h in range(heads):
        cols = slice(h * HEAD_DIM, (h + 1) * HEAD_DIM)
        vals = slice(half + h * HEAD_DIM, half + (h + 1) * HEAD_DIM)
        queries = jnp.concatenate([q_far[0, :, cols], q_near[0, :, cols], pad], axis=0)
        scores = []
        for (by_y, at), block in zip(kinds, blocks, strict=True):
            s = lax.dot_general(
                block[:, cols], queries, (((1,), (1,)), ((), ())), preferred_element_type=F32
            )
            count = block.shape[0]
            text = at + count - rows
            if text > 0:
                eighth = text // 2
                index = lax.broadcasted_iota(jnp.int32, (text, width), 0)
                origin = lax.rem(plane + lax.div(index, eighth), PLANES)
                slot = (
                    lax.rem(y + by_y, row_count) * (PLANES * eighth)
                    + origin * eighth
                    + lax.rem(index, eighth)
                )
                tail = jnp.where(slot < live, s[count - text :], -1e30)
                s = jnp.concatenate([s[: count - text], tail], axis=0)
            scores.append(s)
        top = functools.reduce(
            jnp.maximum, [jnp.max(s, axis=0, keepdims=True) for s in scores]
        )
        if not first:
            old = stat_in[h : h + 1, :]
            top = jnp.maximum(top, old)
            fade = jnp.exp2((old - top) * factor)
        shift = top * factor
        total = None
        acc = None
        for s, block in zip(scores, blocks, strict=True):
            w = jnp.exp2(s * factor - shift)
            part = jnp.sum(w, axis=0, keepdims=True)
            total = part if total is None else total + part
            out = lax.dot_general(
                block[:, vals],
                w.astype(BF16),
                (((0,), (0,)), ((), ())),
                preferred_element_type=F32,
            )
            acc = out if acc is None else acc + out
        span = slice(h * HEAD_DIM, (h + 1) * HEAD_DIM)
        if not first:
            total = total + fade * stat_in[heads + h : heads + h + 1, :]
            acc = acc + fade * acc_in[span, :]
        if last:
            far_out, near_out, log_out = refs
            result = jnp.transpose(acc / total)
            far_out[:rows, cols] = result[:rows].astype(BF16)
            near_out[:, cols] = result[rows : 2 * rows]
            logs.append(shift + jnp.log2(total))
        else:
            acc_out, stat_out = refs
            acc_out[span, :] = acc
            stat_out[h : h + 1, :] = top
            stat_out[heads + h : heads + h + 1, :] = total
    if last:
        log = jnp.concatenate(logs + [jnp.zeros((8 - heads, width), F32)], axis=0)
        log_out[...] = log
        rest = log
        for n in range(3):
            term = rest.astype(BF16)
            rest = rest - term.astype(F32)
            far_out[rows:, n * 256 : (n + 1) * 256] = term[:, :256]


def attend(row_count, live, q_near, q_far, blocks, state, last):
    rows, half = q_near.shape[1:]
    heads = half // HEAD_DIM
    width = pl.cdiv(2 * rows, 128) * 128
    kinds = tuple((by_y, at) for _, by_y, at in blocks)
    if last:
        out_shape = (
            jax.ShapeDtypeStruct((rows + 8, half), BF16),
            jax.ShapeDtypeStruct((rows, half), F32),
            jax.ShapeDtypeStruct((8, width), F32),
        )
    else:
        out_shape = (
            jax.ShapeDtypeStruct((half, width), F32),
            jax.ShapeDtypeStruct((16, width), F32),
        )
    keys = sum(b.shape[0] for b, _, _ in blocks)
    args = [live, q_near, q_far] + [b for b, _, _ in blocks] + list(state or ())
    return call(
        functools.partial(attend_body, kinds, state is None, last, row_count),
        out_shape,
        [SMEM] + [VMEM] * (len(args) - 1),
        (4 * keys * width * half, sum(a.size * 2 for a in args), keys * width * heads),
    )(*args)


def merge_body(x_size, got, near, log, gates, out, gate_out):
    blocks, _, gate_width = gates.shape
    z_size = blocks // x_size
    me = lax.axis_index("dp")
    first = lax.axis_index("head") * (blocks // 2)
    for j in range(blocks // 2):
        by_x = lax.rem(lax.rem(me, x_size) - lax.rem(first + j, x_size) + x_size, x_size)
        by_z = lax.rem(lax.div(me, x_size) - lax.div(first + j, x_size) + z_size, z_size)
        gate_out[:, j * gate_width : (j + 1) * gate_width] = gates[by_x * z_size + by_z]
    rows, half = near.shape
    terms = [got[rows:, n * 256 : (n + 1) * 256].astype(F32) for n in range(3)]
    theirs = jnp.transpose(terms[0] + terms[1] + terms[2])
    mine = jnp.transpose(log[...])
    for h in range(half // HEAD_DIM):
        cols = slice(h * HEAD_DIM, (h + 1) * HEAD_DIM)
        a = mine[rows : 2 * rows, h : h + 1]
        b = theirs[:rows, h : h + 1]
        share = 1.0 / (1.0 + jnp.exp2(jnp.minimum(b - a, 126.0)))
        out[:, cols] = (
            near[:, cols] * share + got[:rows, cols].astype(F32) * (1.0 - share)
        ).astype(BF16)


def project_first_body(mine, w_own, out):
    out[...] = jnp.dot(mine[...], w_own[...], preferred_element_type=F32)


def project_last_body(partial, theirs, w_got, gate, out):
    total = partial[...] + jnp.dot(theirs[...], w_got[...], preferred_element_type=F32)
    out[0] = (total * gate[...]).astype(BF16)


def gather_gates(gate, x_size, z_size):
    def along(array, by_z, by_x):
        pairs = [
            (z * x_size + x, (z + by_z) % z_size * x_size + (x + by_x) % x_size)
            for z in range(z_size)
            for x in range(x_size)
        ]
        return lax.ppermute(array, "dp", pairs)

    own = gate.reshape(1, 1, gate.shape[0])
    held = jnp.concatenate([own] + [along(own, i, 0) for i in range(1, z_size)], axis=0)
    step = 1
    while step < x_size:
        held = jnp.concatenate([held, along(held, 0, step)], axis=0)
        step *= 2
    return held


def per_device(q_img, k_img, v_img, k_txt, v_txt, text_length, w_out, branch_gate):
    row_count = lax.axis_size("seq") // PLANES
    rows, width = q_img.shape[1:]
    text = k_txt.shape[1] // 2
    k_img, v_img, k_txt, v_txt = (
        pltpu.with_memory_space_constraint(x, pltpu.HBM) for x in (k_img, v_img, k_txt, v_txt)
    )

    def shape(*dims):
        return jax.ShapeDtypeStruct(dims, BF16)

    t_send = call(
        text_body, shape(text, 2 * width), [HBM] * 2, (0, 8 * text * width, 0), copies=2
    )(k_txt, v_txt)
    t_got = move(t_send, row_count, 0, -1)
    block = call(
        pack_body,
        shape(rows + 2 * text, 2 * width),
        [HBM] * 4 + [VMEM],
        (0, 8 * rows * width, 0),
        copies=4,
    )(k_img, v_img, k_txt, v_txt, t_got)
    q_got = move(q_img, row_count, 0, 2)

    up, down = [block], [block]
    for _ in range(1, 4):
        up.append(move(up[-1], row_count, 1, 0))
        down.append(move(down[-1], row_count, -1, 0))
    cut = (rows + 2 * text) * 3 // 4
    up.append(move(up[3][:cut], row_count, 1, 0))
    down.append(move(down[3][cut:], row_count, -1, 0))

    groups = [
        [(block, 0, 0), (up[1], -1, 0), (down[1], 1, 0)],
        [(up[2], -2, 0), (down[2], 2, 0)],
        [(up[3], -3, 0), (down[3], 3, 0)],
        [(up[4], -4, 0), (down[4], 4, cut)],
    ]
    state = None
    for n, group in enumerate(groups):
        blocks = [(b, by % row_count, at) for b, by, at in group]
        state = attend(row_count, text_length, q_img, q_got, blocks, state, n == len(groups) - 1)
    o_far, o_near, o_log = state

    core = lax.axis_index("head")
    out_width = w_out.shape[1] // 2
    w_send = lax.dynamic_slice_in_dim(w_out, (1 - core) * out_width, out_width, 1)
    w_own = lax.dynamic_slice_in_dim(w_out, core * out_width, out_width, 1)
    w_got = swap_cores(w_send)
    gates = gather_gates(branch_gate, 4, lax.axis_size("dp") // 4)

    o_got = move(o_far, row_count, 0, 2)
    mine, gate = call(
        functools.partial(merge_body, 4),
        (shape(rows, width), jax.ShapeDtypeStruct((1, out_width), F32)),
        [VMEM] * 4,
        (0, 8 * rows * width, 0),
    )(o_got, o_near, o_log, gates)
    theirs = swap_cores(mine)
    partial = call(
        project_first_body,
        jax.ShapeDtypeStruct((rows, out_width), F32),
        [VMEM] * 2,
        (2 * rows * width * out_width, 2 * width * out_width, 0),
    )(mine, w_own)
    return call(
        project_last_body,
        shape(1, rows, out_width),
        [VMEM] * 4,
        (2 * rows * width * out_width, 2 * width * out_width, 0),
    )(partial, theirs, w_got, gate)


def solution(mesh):
    in_specs = (
        P("dp", "seq", "head"),
        P("dp", "seq", "head"),
        P("dp", "seq", "head"),
        P("dp", "seq", "head"),
        P("dp", "seq", "head"),
        P("dp", None),
        P("head", None),
        P("dp"),
    )
    out_specs = P("dp", "seq", "head")
    return jax.shard_map(
        per_device, mesh=mesh, in_specs=in_specs, out_specs=out_specs, check_vma=False
    )
```
